256 devices in a mesh: dp: 4 (over x), expert: 64 (over z, y, core).
Axes of the slice: x: 4, y: 4, z: 8, core: 2. Of those that a mesh axis runs over, the one named last changes fastest.
Arguments:
- hidden_acts: bfloat16 [4, 64, 1024, 768], P('dp', 'expert'), may hold values from -6 to 6
- out_grads: bfloat16 [4, 64, 1024, 2048], P('dp', 'expert'), may hold values from -0.29882812 to 0.29882812
- row_counts: int32 [4, 64], P('dp', 'expert'), may hold values from 128 to 1024, as said below
- plan_now: int32 [4, 64], replicated, may hold values from 0 to 23, as said below
- plan_next: int32 [4, 64], replicated, may hold values from 0 to 23, as said below
- master: float32 [24, 768, 2048], P(None, 'expert', 'dp'), may hold values from -6 to 6
- moment_one: float32 [24, 768, 2048], P(None, 'expert', 'dp'), may hold values from -6 to 6
- moment_two: float32 [24, 768, 2048], P(None, 'expert', 'dp'), may hold values from 0.01 to 0.3
Outputs:
- master_new: float32 [24, 768, 2048], P(None, 'expert', 'dp')
- moment_one_new: float32 [24, 768, 2048], P(None, 'expert', 'dp')
- moment_two_new: float32 [24, 768, 2048], P(None, 'expert', 'dp')
- replica_weights: bfloat16 [4, 64, 768, 2048], P('dp', 'expert')
The draws below stay inside these ranges and needn't reach their ends.
Inputs may be any that keep to these rules, and one draw needn't show every extreme that they name: `plan_now`: every expert is named by 1 to 16 devices, and some expert by exactly 16. `plan_next`: every expert is named by 1 to 16 devices, and some expert by exactly 16. `row_counts`: A multiple of 128; rows from it on are padding. Some device has all 1024 rows live.
All inputs are finite; a program needn't handle non-finite values.
Results may differ from the reference program's by a relative error of at most 0.005.
Values may be sent and summed in bfloat16 or wider, within the bound.
A program may use at most 64 MiB of HBM per device.

```python
import math
import jax
import jax.numpy as jnp
from jax import lax

FF = 768
DW = 2048
ROWS = 1024
MAXREP = 16
GROUPS = 4
OWNERS = 64
SLOTS = 256
EXPERTS = 24


def replica_plan(seed_key):
    count_keys = jax.random.split(jax.random.fold_in(seed_key, 11), EXPERTS)

    def choose(remain, item):
        position, subkey = item
        later = EXPERTS - 1 - position
        lowest = jnp.maximum(1, remain - MAXREP * later)
        highest = jnp.minimum(MAXREP, remain - later)
        drawn = jax.random.randint(subkey, (), lowest, highest + 1, dtype=jnp.int32)
        taken = jnp.where(position == 0, MAXREP, drawn).astype(jnp.int32)
        return (remain - taken, taken)
    unused, counts = lax.scan(choose, jnp.int32(SLOTS), (jnp.arange(EXPERTS, dtype=jnp.int32), count_keys))
    order = jax.random.permutation(jax.random.fold_in(seed_key, 12), EXPERTS)
    counts = counts[order]
    bounds = jnp.cumsum(counts)
    positions = jnp.arange(SLOTS, dtype=jnp.int32)
    owner = jnp.sum((positions[:, None] >= bounds[None, :]).astype(jnp.int32), axis=1)
    owner = jax.random.permutation(jax.random.fold_in(seed_key, 13), owner)
    return owner.reshape(GROUPS, OWNERS).astype(jnp.int32)


def draw_plan_now(key, part):
    return replica_plan(jax.random.fold_in(key, 7))


def draw_plan_next(key, part):
    return replica_plan(jax.random.fold_in(key, 101))


def draw_row_counts(key, part):
    blocks = jax.random.randint(jax.random.fold_in(key, 21), (SLOTS,), 1, ROWS // 128 + 1, dtype=jnp.int32)
    chosen = jax.random.randint(jax.random.fold_in(key, 22), (), 0, SLOTS, dtype=jnp.int32)
    blocks = jnp.where(jnp.arange(SLOTS, dtype=jnp.int32) == chosen, ROWS // 128, blocks)
    return (blocks * 128).reshape(GROUPS, OWNERS).astype(jnp.int32)


def shard_levels(key, shape, cuts, low, top_value):
    loudness, own = 1.0, jax.random.fold_in(key, 6)
    for axis_at, parts in cuts:
        steps = jnp.exp(jax.random.uniform(jax.random.fold_in(own, axis_at), (parts,), jnp.float32, low / len(cuts), top_value / len(cuts)))
        loudness = loudness * jnp.repeat(steps, shape[axis_at] // parts).reshape([-1 if axis == axis_at else 1 for axis in range(len(shape))])
    return loudness


def bell_draw(stream_key, extent, spread, most, pieces=(), kind=jnp.bfloat16):
    values = jax.random.normal(stream_key, extent, jnp.float32) * spread
    if len(pieces) > 0:
        values = shard_levels(stream_key, extent, pieces, -0.22, 0.18) * values
    return jnp.clip(values, min=-most, max=most).astype(kind)


def setup_inputs(seed: int = 0) -> dict:
    key_of = jax.random.split(jax.random.key(seed), 9)
    return {
        "hidden_acts": bell_draw(key_of[0], (GROUPS, OWNERS, ROWS, FF), 1.0, 6.0, ((0, 4), (1, 64))),
        "out_grads": bell_draw(key_of[1], (GROUPS, OWNERS, ROWS, DW), 0.05, 0.29882812, ((0, 4), (1, 64))),
        "row_counts": draw_row_counts(jax.random.fold_in(key_of[8], 71), 0),
        "plan_now": draw_plan_now(jax.random.fold_in(key_of[8], 71), 0),
        "plan_next": draw_plan_next(jax.random.fold_in(key_of[8], 71), 0),
        "master": bell_draw(key_of[5], (EXPERTS, FF, DW), 1.0, 6.0, ((1, 64), (2, 4)), jnp.float32),
        "moment_one": bell_draw(key_of[6], (EXPERTS, FF, DW), 1.0, 6.0, ((1, 64), (2, 4)), jnp.float32),
        "moment_two": jnp.clip(jnp.exp(math.log(0.3) - 3.4011974 * jax.random.uniform(key_of[7], (EXPERTS, FF, DW), jnp.float32) ** shard_levels(key_of[7], (EXPERTS, FF, DW), ((1, 64), (2, 4)), -0.2, 0.2)), 0.01, 0.3),
    }


beta_one = 0.9
beta_two = 0.999
learn_rate = 0.1
epsilon = 1e-08
first_fix = 1.0 - beta_one ** 10
second_fix = 1.0 - beta_two ** 10

def reference(hidden_acts, out_grads, row_counts, plan_now, plan_next, master, moment_one, moment_two):
    row_index = jnp.arange(ROWS, dtype=jnp.int32)
    inputs = (hidden_acts.reshape(SLOTS, ROWS, FF), out_grads.reshape(SLOTS, ROWS, DW), row_counts.reshape(SLOTS), plan_now.reshape(SLOTS))

    def accumulate(running, item):
        hidden, upstream, count, expert = item
        row_mask = (row_index < count).astype(hidden.dtype)[:, None]
        partial_value = lax.dot_general(hidden * row_mask, upstream, (((0,), (0,)), ((), ())), preferred_element_type=jnp.float32).astype(jnp.bfloat16)
        partial_value = lax.optimization_barrier(partial_value)
        current = lax.dynamic_index_in_dim(running, expert, 0, keepdims=False)
        running = lax.dynamic_update_index_in_dim(running, current + partial_value.astype(jnp.float32), expert, 0)
        return (running, None)
    grad_sum, unused = lax.scan(accumulate, jnp.zeros((EXPERTS, FF, DW), jnp.float32), inputs)
    moment_one_new = beta_one * moment_one + (1.0 - beta_one) * grad_sum
    moment_two_new = beta_two * moment_two + (1.0 - beta_two) * grad_sum * grad_sum
    master_new = master - learn_rate * (moment_one_new / first_fix) / (jnp.sqrt(moment_two_new / second_fix) + epsilon)
    rounded = master_new.astype(jnp.bfloat16)
    replica_weights = jnp.take(rounded, plan_next, axis=0)
    return (master_new, moment_one_new, moment_two_new, replica_weights)
```

```python
import functools

import jax
import jax.numpy as jnp
from jax import lax
from jax.experimental import pallas as pl
from jax.experimental.pallas import tpu as pltpu
from jax.sharding import PartitionSpec as P

beta_one = 0.9
beta_two = 0.999
learn_rate = 0.1
epsilon = 1e-08
first_fix = 1.0 - beta_one**10
second_fix = 1.0 - beta_two**10

MESH = pl.DeviceIdType.MESH
BF16 = jnp.bfloat16
F32 = jnp.float32
EXPERTS = 24
PLANE = 32
OUT_GROUPS = ((0, 1), (1, 3), (3, 5), (5, 8))
IN_GROUPS = ((0, 1), (1, 3), (3, 5), (5, 7), (7, 8))


def place():
    o = lax.axis_index("expert")
    return lax.axis_index("dp"), o // 8, lax.rem(o // 2, 4), lax.rem(o, 2)


def device(x, z, y, c):
    return (x, z * 8 + y * 2 + c)


def peer(index):
    x, z, y, c = place()
    t = lax.rem(index, 4)
    dx = lax.rem(1 + 2 * t + t // 2, 4)
    dy = lax.rem(dx + 1 + lax.rem(index // 4, 4), 4)
    dc = 1 - index // 16
    return lax.rem(x + dx, 4), lax.rem(y + dy, 4), lax.rem(c + dc, 2)


def meet():
    x, z, y, c = place()
    barrier = pltpu.get_barrier_semaphore()

    @pl.loop(0, PLANE - 1)
    def _(index):
        px, py, pc = peer(index)
        pl.semaphore_signal(barrier, inc=1, device_id=device(px, z, py, pc), device_id_type=MESH)

    for step in (1, 7):
        pl.semaphore_signal(
            barrier, inc=1, device_id=device(x, lax.rem(z + step, 8), y, c), device_id_type=MESH
        )
    return barrier


def all_met(barrier):
    pl.semaphore_wait(barrier, PLANE + 1)


def remote(src, dst, send_sem, recv_sem, target):
    return pltpu.make_async_remote_copy(
        src_ref=src, dst_ref=dst, send_sem=send_sem, recv_sem=recv_sem, device_id=target, device_id_type=MESH
    )


def drain(ref, sem):
    pltpu.make_async_copy(ref, ref, sem).wait()


def reduce_kernel(
    count, prev, last, hid, grd, own,
    hid_t, part, pieces, acc, up_s, up_r, down_s, down_r, total, swap_s, swap_r,
    plane_send, plane_recv, self_sem, ring_send, ring_recv, swap_sem,
):
    x, z, y, c = place()
    slot = (x * 4 + y) * 2 + c
    barrier = meet()
    rows = hid.shape[0]
    live = lax.broadcasted_iota(jnp.int32, (256, 1), 0)

    for k in range(rows // 256):
        block = hid[k * 256 : (k + 1) * 256, :]
        kept = jnp.where(live + k * 256 < count[0, 0], block.astype(F32), 0.0)
        hid_t[:, k * 256 : (k + 1) * 256] = kept.T.astype(BF16)

    def multiply(half):
        for px in range(4):
            col = px * 512 + half * 128
            rhs = jnp.concatenate([grd[:, col : col + 128], grd[:, col + 256 : col + 384]], axis=1)
            out = jnp.dot(hid_t[...], rhs, preferred_element_type=F32)
            for dest in range(8):
                away = lax.rem(dest - z + 8, 8)
                pos = jnp.where(away == 0, 7, jnp.where(away < 4, 7 - 2 * away, 2 * (away - 4)))
                for py in range(4):
                    top = dest * 96 + py * 24
                    block = out[top : top + 24, :].astype(BF16)
                    part[pos, py, :, col : col + 128] = block[:, :128]
                    part[pos, py, :, col + 256 : col + 384] = block[:, 128:]

    def spread(half):
        for g, (a, b) in enumerate(OUT_GROUPS):

            @pl.loop(0, PLANE - 1)
            def _(index):
                px, py, pc = peer(index)
                col = pl.multiple_of(px * 512 + pc * 256 + half * 128, 128)
                remote(
                    part.at[a:b, py, :, pl.ds(col, 128)],
                    pieces.at[half, slot, a:b],
                    plane_send.at[half],
                    plane_recv.at[half, g],
                    device(px, z, py, pc),
                ).start()

        col = pl.multiple_of(x * 512 + c * 256 + half * 128, 128)
        pltpu.make_async_copy(
            part.at[:, y, :, pl.ds(col, 128)], pieces.at[half, slot], self_sem.at[half]
        ).start()

    def gather_up(half):
        zplus, zminus = lax.rem(z + 1, 8), lax.rem(z + 7, 8)
        acc[PLANE] = jnp.zeros_like(acc[PLANE])
        drain(pieces.at[half, 0], self_sem.at[half])
        for g, (a, b) in enumerate(OUT_GROUPS):
            drain(pieces.at[half, pl.ds(0, PLANE - 1), a:b], plane_recv.at[half, g])

            @pl.loop(0, PLANE)
            def _(i):
                acc[i, a:b] = pieces[half, i, a:b].astype(F32) + acc[prev[i], a:b]

            if g == 0:

                @pl.loop(0, EXPERTS // 2)
                def _(e):
                    up_s[half, 0, e] = acc[last[e], 0].astype(BF16)
                    down_s[half, 0, e] = acc[last[e + 12], 0].astype(BF16)

            else:
                for ring, (buf, r) in enumerate(((up_s, up_r), (down_s, down_r))):
                    first = half_of(ring) if g == 1 else slice(0, EXPERTS)
                    n = first.stop - first.start
                    drain(r.at[half, g - 1, pl.ds(0, n)], ring_recv.at[half, ring, g - 1])
                    pos = a + ring

                    @pl.loop(0, n)
                    def _(e):
                        buf[half, g, e + first.start] = (
                            acc[last[e + first.start], pos] + r[half, g - 1, e].astype(F32)
                        ).astype(BF16)

                    if g == 1:

                        @pl.loop(0, EXPERTS - n)
                        def _(e):
                            other = e + (12 - first.start)
                            buf[half, g, other] = acc[last[other], pos].astype(BF16)

            n = 12 if g == 0 else EXPERTS
            for ring, (s, r, to) in enumerate(((up_s, up_r, zplus), (down_s, down_r, zminus))):
                remote(
                    s.at[half, g, pl.ds(0, n)],
                    r.at[half, g, pl.ds(0, n)],
                    ring_send.at[half, ring, g],
                    ring_recv.at[half, ring, g],
                    device(x, to, y, c),
                ).start()

        for ring, r in enumerate((up_r, down_r)):
            drain(r.at[half, 3], ring_recv.at[half, ring, 3])

        @pl.loop(0, EXPERTS)
        def _(e):
            total[half, e] = acc[last[e], 7] + up_r[half, 3, e].astype(F32) + down_r[half, 3, e].astype(F32)

        col = pl.multiple_of(c * 256 + half * 128, 128)

        @pl.loop(0, EXPERTS)
        def _(e):
            low, high = total[half, e, 0:12, :], total[half, e, 12:24, :]
            own[e, :, pl.ds(col, 128)] = jnp.where(c == 0, low, high)
            swap_s[half, e] = jnp.where(c == 0, high, low)

        remote(
            swap_s.at[half], swap_r.at[half], swap_sem.at[half, 0], swap_sem.at[half, 1], device(x, z, y, 1 - c)
        ).start()

    multiply(0)
    all_met(barrier)
    spread(0)
    multiply(1)
    spread(1)
    gather_up(0)
    gather_up(1)
    for half in range(2):
        drain(swap_r.at[half], swap_sem.at[half, 1])
        col = pl.multiple_of((1 - c) * 256 + half * 128, 128)
        own[:, :, pl.ds(col, 128)] = swap_r[half]
    for half in range(2):
        drain(swap_s.at[half], swap_sem.at[half, 0])
        drain(pieces.at[half, pl.ds(0, PLANE - 1)], plane_send.at[half])
        for g in range(4):
            n = 12 if g == 0 else EXPERTS
            for ring, s in enumerate((up_s, down_s)):
                drain(s.at[half, g, pl.ds(0, n)], ring_send.at[half, ring, g])


def half_of(ring):
    return slice(12 * ring, 12 * ring + 12)


def expand_kernel(
    plan, new, out,
    swap_r, whole, held_00, held_01, held_02, held_03, held_04, held_10, held_11, held_12, held_13, held_14,
    picked, result,
    swap_sem, ring_send, ring_recv, plane_send, plane_recv, out_sem,
):
    held = ((held_00, held_01, held_02, held_03, held_04), (held_10, held_11, held_12, held_13, held_14))
    x, z, y, c = place()
    zplus, zminus = lax.rem(z + 1, 8), lax.rem(z + 7, 8)
    barrier = meet()
    all_met(barrier)
    for half in range(2):
        col = pl.multiple_of((1 - c) * 256 + half * 128, 128)
        remote(
            new.at[:, :, pl.ds(col, 128)],
            swap_r.at[half],
            swap_sem.at[half, 0],
            swap_sem.at[half, 1],
            device(x, z, y, 1 - c),
        ).start()
    for half in range(2):
        drain(swap_r.at[half], swap_sem.at[half, 1])
        col = pl.multiple_of(c * 256 + half * 128, 128)

        @pl.loop(0, EXPERTS)
        def _(e):
            mine, theirs = new[e, :, pl.ds(col, 128)], swap_r[half, e]
            whole[half, e, 0:12, :] = jnp.where(c == 0, mine, theirs)
            whole[half, e, 12:24, :] = jnp.where(c == 0, theirs, mine)

        held[half][0][0] = whole[half].astype(BF16)

    def hop(half, k):
        for ring, to in enumerate((zplus, zminus)):
            src = 0 if k == 0 else ring
            dst = 0 if k == 3 else ring
            part = pl.ds(12 * ring, 12) if k == 3 else pl.ds(0, EXPERTS)
            yield remote(
                held[half][k].at[src, part],
                held[half][k + 1].at[dst, part],
                ring_send.at[half, ring, k],
                ring_recv.at[half, ring, k],
                device(x, to, y, c),
            )

    for half in range(2):
        for copy in hop(half, 0):
            copy.start()
    for g, (a, b) in enumerate(IN_GROUPS):
        for half in range(2):
            if g:
                for copy in hop(half, g - 1):
                    copy.wait_recv()
                if g < 4:
                    for copy in hop(half, g):
                        copy.start()
            col = pl.multiple_of(x * 512 + c * 256 + half * 128, 128)

            @pl.loop(0, PLANE - 1)
            def _(index):
                px, py, pc = peer(index)
                e = plan[px, z * 8 + py * 2 + pc]
                picked[half, index, a:b] = held[half][g][:, e]
                remote(
                    picked.at[half, index, a:b],
                    result.at[a:b, y, :, pl.ds(col, 128)],
                    plane_send.at[half],
                    plane_recv.at[g],
                    device(px, z, py, pc),
                ).start()

            result[a:b, y, :, pl.ds(col, 128)] = held[half][g][:, plan[x, z * 8 + y * 2 + c]]
    for g, (a, b) in enumerate(IN_GROUPS):
        drain(picked.at[:, pl.ds(0, PLANE - 1), a:b], plane_recv.at[g])
        for pos in range(a, b):
            away = (0, 7, 1, 6, 2, 5, 3, 4)[pos]
            pltpu.make_async_copy(result.at[pos], out.at[lax.rem(z + away, 8)], out_sem.at[pos]).start()
    for pos in range(8):
        drain(result.at[pos], out_sem.at[pos])
    for half in range(2):
        drain(swap_r.at[half], swap_sem.at[half, 0])
        drain(picked.at[half, pl.ds(0, PLANE - 1)], plane_send.at[half])
        for k in range(4):
            for copy in hop(half, k):
                copy.wait_send()


VMEM = pl.BlockSpec(memory_space=pltpu.VMEM)
SMEM = pl.BlockSpec(memory_space=pltpu.SMEM)
ANY = pl.BlockSpec(memory_space=pl.ANY)
DMA = pltpu.SemaphoreType.DMA


def params(number):
    return pltpu.CompilerParams(collective_id=number, has_side_effects=True, vmem_limit_bytes=60 * 2**20)


def reduce_grads(count, prev, last, hidden, upstream):
    block = (24, 24, 128)
    return pl.pallas_call(
        reduce_kernel,
        out_shape=jax.ShapeDtypeStruct((24, 12, 512), F32),
        in_specs=[SMEM, SMEM, SMEM, VMEM, VMEM],
        out_specs=VMEM,
        scratch_shapes=[
            pltpu.VMEM((768, 1024), BF16),
            pltpu.VMEM((8, 4, 24, 2048), BF16),
            pltpu.VMEM((2, 32, 8, 24, 128), BF16),
            pltpu.VMEM((33, 8, 24, 128), F32),
        ]
        + [pltpu.VMEM((2, 4) + block, BF16)] * 4
        + [
            pltpu.VMEM((2,) + block, F32),
            pltpu.VMEM((2, 24, 12, 128), F32),
            pltpu.VMEM((2, 24, 12, 128), F32),
            DMA((2,)),
            DMA((2, 4)),
            DMA((2,)),
            DMA((2, 2, 4)),
            DMA((2, 2, 4)),
            DMA((2, 2)),
        ],
        compiler_params=params(0),
        name="reduce_grads",
    )(count, prev, last, hidden, upstream)


def expand_weights(plan_next, master_new):
    return pl.pallas_call(
        expand_kernel,
        out_shape=jax.ShapeDtypeStruct((8, 4, 24, 2048), BF16),
        in_specs=[SMEM, VMEM],
        out_specs=ANY,
        scratch_shapes=[
            pltpu.VMEM((2, 24, 12, 128), F32),
            pltpu.VMEM((2, 24, 24, 128), F32),
        ]
        + [pltpu.VMEM((b - a, 24, 24, 128), BF16) for _ in range(2) for a, b in IN_GROUPS]
        + [
            pltpu.VMEM((2, 31, 8, 24, 128), BF16),
            pltpu.VMEM((8, 4, 24, 2048), BF16),
            DMA((2, 2)),
            DMA((2, 2, 4)),
            DMA((2, 2, 4)),
            DMA((2,)),
            DMA((5,)),
            DMA((8,)),
        ],
        compiler_params=params(1),
        name="expand_weights",
    )(plan_next, master_new)


def per_device(hidden_acts, out_grads, row_counts, plan_now, plan_next, master, moment_one, moment_two):
    z = lax.axis_index("expert") // 8
    ids = lax.dynamic_slice_in_dim(plan_now, z * 8, 8, axis=1).reshape(PLANE)
    order = jnp.arange(PLANE, dtype=jnp.int32)
    earlier = (ids[None, :] == ids[:, None]) & (order[None, :] < order[:, None])
    prev = jnp.max(jnp.where(earlier, order[None, :], -1), axis=1)
    prev = jnp.where(prev < 0, PLANE, prev)
    named = ids[None, :] == jnp.arange(EXPERTS, dtype=jnp.int32)[:, None]
    last = jnp.max(jnp.where(named, order[None, :], -1), axis=1)
    last = jnp.where(last < 0, PLANE, last)
    grad_sum = reduce_grads(row_counts, prev, last, hidden_acts[0, 0], out_grads[0, 0])
    moment_one_new = beta_one * moment_one + (1.0 - beta_one) * grad_sum
    moment_two_new = beta_two * moment_two + (1.0 - beta_two) * grad_sum * grad_sum
    master_new = master - learn_rate * (moment_one_new / first_fix) / (
        jnp.sqrt(moment_two_new / second_fix) + epsilon
    )
    replica = expand_weights(plan_next, master_new)
    return (master_new, moment_one_new, moment_two_new, replica.reshape(1, 1, 768, 2048))


def solution(mesh):
    state = P(None, "expert", "dp")
    split = P("dp", "expert", None, None)
    return jax.shard_map(
        per_device,
        mesh=mesh,
        in_specs=(split, split, P("dp", "expert"), P(), P(), state, state, state),
        out_specs=(state, state, state, split),
        check_vma=False,
    )
```

```python
import functools

import jax
import jax.numpy as jnp
from jax import lax
from jax.experimental import pallas as pl
from jax.experimental.pallas import tpu as pltpu
from jax.sharding import PartitionSpec as P

beta_one = 0.9
beta_two = 0.999
learn_rate = 0.1
epsilon = 1e-08
first_fix = 1.0 - beta_one**10
second_fix = 1.0 - beta_two**10

MESH = pl.DeviceIdType.MESH
BF16 = jnp.bfloat16
F32 = jnp.float32
EXPERTS = 24
PLANE = 32
OUT_GROUPS = ((0, 1), (1, 3), (3, 5), (5, 8))
IN_GROUPS = ((0, 1), (1, 3), (3, 5), (5, 7), (7, 8))


def place():
    o = lax.axis_index("expert")
    return lax.axis_index("dp"), o // 8, lax.rem(o // 2, 4), lax.rem(o, 2)


def device(x, z, y, c):
    return (x, z * 8 + y * 2 + c)


def peer(index):
    x, z, y, c = place()
    t = lax.rem(index, 4)
    dx = lax.rem(1 + 2 * t + t // 2, 4)
    dy = lax.rem(dx + 1 + lax.rem(index // 4, 4), 4)
    dc = 1 - index // 16
    return lax.rem(x + dx, 4), lax.rem(y + dy, 4), lax.rem(c + dc, 2)


def meet():
    x, z, y, c = place()
    barrier = pltpu.get_barrier_semaphore()

    @pl.loop(0, PLANE - 1)
    def _(index):
        px, py, pc = peer(index)
        pl.semaphore_signal(barrier, inc=1, device_id=device(px, z, py, pc), device_id_type=MESH)

    for step in (1, 7):
        pl.semaphore_signal(
            barrier, inc=1, device_id=device(x, lax.rem(z + step, 8), y, c), device_id_type=MESH
        )
    return barrier


def all_met(barrier):
    pl.semaphore_wait(barrier, PLANE + 1)


def remote(src, dst, send_sem, recv_sem, target):
    return pltpu.make_async_remote_copy(
        src_ref=src, dst_ref=dst, send_sem=send_sem, recv_sem=recv_sem, device_id=target, device_id_type=MESH
    )


def drain(ref, sem):
    pltpu.make_async_copy(ref, ref, sem).wait()


def adam(grad, weight, first, second):
    first = beta_one * first + (1.0 - beta_one) * grad
    second = beta_two * second + (1.0 - beta_two) * grad * grad
    step = learn_rate * (first / first_fix) / (jnp.sqrt(second / second_fix) + epsilon)
    return weight - step, first, second


def half_of(ring):
    return slice(12 * ring, 12 * ring + 12)


def kernel(
    count, prev, last, plan, hid_in, grd_in, weight_in, first_in, second_in, own, out,
    hid, grd, hid_t, part, pieces, acc, up_s, up_r, down_s, down_r, total, swap_s, swap_r,
    load_0, load_1, load_2, state, kept_grad, mine, back_s, back_r, whole,
    held_00, held_01, held_02, held_03, held_04, held_10, held_11, held_12, held_13, held_14,
    picked, result,
    load_sem, plane_send, plane_recv, self_sem, ring_send, ring_recv, swap_sem, back_sem,
    gather_send, gather_recv, spread_send, spread_recv, out_sem,
):
    held = ((held_00, held_01, held_02, held_03, held_04), (held_10, held_11, held_12, held_13, held_14))
    loads = (load_0, load_1, load_2)
    x, z, y, c = place()
    zplus, zminus = lax.rem(z + 1, 8), lax.rem(z + 7, 8)
    slot = (x * 4 + y) * 2 + c
    rows = hid.shape[0]
    copies = [pltpu.make_async_copy(hid_in, hid, load_sem.at[0]), pltpu.make_async_copy(grd_in, grd, load_sem.at[1])]
    for i, ref in enumerate((weight_in, first_in, second_in)):
        copies.append(pltpu.make_async_copy(ref, loads[i], load_sem.at[2 + i]))
    for copy in copies:
        copy.start()
    barrier = meet()
    live = lax.broadcasted_iota(jnp.int32, (256, 1), 0)
    copies[0].wait()

    for k in range(rows // 256):
        block = hid[k * 256 : (k + 1) * 256, :]
        kept = jnp.where(live + k * 256 < count[0, 0], block.astype(F32), 0.0)
        hid_t[:, k * 256 : (k + 1) * 256] = kept.T.astype(BF16)
    copies[1].wait()

    def multiply(half):
        for px in range(4):
            col = px * 512 + half * 128
            rhs = jnp.concatenate([grd[:, col : col + 128], grd[:, col + 256 : col + 384]], axis=1)
            out = jnp.dot(hid_t[...], rhs, preferred_element_type=F32)
            for dest in range(8):
                away = lax.rem(dest - z + 8, 8)
                pos = jnp.where(away == 0, 7, jnp.where(away < 4, 7 - 2 * away, 2 * (away - 4)))
                for py in range(4):
                    top = dest * 96 + py * 24
                    block = out[top : top + 24, :].astype(BF16)
                    part[pos, py, :, col : col + 128] = block[:, :128]
                    part[pos, py, :, col + 256 : col + 384] = block[:, 128:]

    def spread(half):
        for g, (a, b) in enumerate(OUT_GROUPS):

            @pl.loop(0, PLANE - 1)
            def _(index):
                px, py, pc = peer(index)
                col = pl.multiple_of(px * 512 + pc * 256 + half * 128, 128)
                remote(
                    part.at[a:b, py, :, pl.ds(col, 128)],
                    pieces.at[half, slot, a:b],
                    plane_send.at[half],
                    plane_recv.at[half, g],
                    device(px, z, py, pc),
                ).start()

        col = pl.multiple_of(x * 512 + c * 256 + half * 128, 128)
        pltpu.make_async_copy(
            part.at[:, y, :, pl.ds(col, 128)], pieces.at[half, slot], self_sem.at[half]
        ).start()

    def add_group(half, g):
        a, b = OUT_GROUPS[g]
        if g == 0:
            drain(pieces.at[half, 0], self_sem.at[half])
        drain(pieces.at[half, pl.ds(0, PLANE - 1), a:b], plane_recv.at[half, g])

        @pl.loop(0, PLANE)
        def _(i):
            acc[i, a:b] = pieces[half, i, a:b].astype(F32) + acc[prev[i], a:b]

        if g == 0:

            @pl.loop(0, EXPERTS // 2)
            def _(e):
                up_s[half, 0, e] = acc[last[e], 0].astype(BF16)
                down_s[half, 0, e] = acc[last[e + 12], 0].astype(BF16)

        else:
            for ring, (buf, r) in enumerate(((up_s, up_r), (down_s, down_r))):
                first = half_of(ring) if g == 1 else slice(0, EXPERTS)
                n = first.stop - first.start
                drain(r.at[half, g - 1, pl.ds(0, n)], ring_recv.at[half, ring, g - 1])
                pos = a + ring

                @pl.loop(0, n)
                def _(e):
                    buf[half, g, e + first.start] = (
                        acc[last[e + first.start], pos] + r[half, g - 1, e].astype(F32)
                    ).astype(BF16)

                if g == 1:

                    @pl.loop(0, EXPERTS - n)
                    def _(e):
                        other = e + (12 - first.start)
                        buf[half, g, other] = acc[last[other], pos].astype(BF16)

        n = 12 if g == 0 else EXPERTS
        for ring, (s, r, to) in enumerate(((up_s, up_r, zplus), (down_s, down_r, zminus))):
            remote(
                s.at[half, g, pl.ds(0, n)],
                r.at[half, g, pl.ds(0, n)],
                ring_send.at[half, ring, g],
                ring_recv.at[half, ring, g],
                device(x, to, y, c),
            ).start()

    def finish_sum(half):
        for ring, r in enumerate((up_r, down_r)):
            drain(r.at[half, 3], ring_recv.at[half, ring, 3])

        @pl.loop(0, EXPERTS)
        def _(e):
            total[half, e] = acc[last[e], 7] + up_r[half, 3, e].astype(F32) + down_r[half, 3, e].astype(F32)

        @pl.loop(0, EXPERTS)
        def _(e):
            low, high = total[half, e, 0:12, :], total[half, e, 12:24, :]
            kept_grad[half, e] = jnp.where(c == 0, low, high)
            swap_s[half, e] = jnp.where(c == 0, high, low)

        remote(
            swap_s.at[half], swap_r.at[half], swap_sem.at[half, 0], swap_sem.at[half, 1], device(x, z, y, 1 - c)
        ).start()

        @pl.loop(0, EXPERTS)
        def _(e):
            at = 2 * c + half
            mine[half, e] = adam(kept_grad[half, e], state[0, at, e], state[1, at, e], state[2, at, e])[0]

    def update(half):
        drain(swap_r.at[half], swap_sem.at[half, 1])

        @pl.loop(0, EXPERTS)
        def _(e):
            at = 2 * (1 - c) + half
            back_s[half, e] = adam(swap_r[half, e], state[0, at, e], state[1, at, e], state[2, at, e])[0]

        remote(
            back_s.at[half], back_r.at[half], back_sem.at[half, 0], back_sem.at[half, 1], device(x, z, y, 1 - c)
        ).start()

    def hop(half, k):
        for ring, to in enumerate((zplus, zminus)):
            src = 0 if k == 0 else ring
            dst = 0 if k == 3 else ring
            piece = pl.ds(12 * ring, 12) if k == 3 else pl.ds(0, EXPERTS)
            yield remote(
                held[half][k].at[src, piece],
                held[half][k + 1].at[dst, piece],
                gather_send.at[half, ring, k],
                gather_recv.at[half, ring, k],
                device(x, to, y, c),
            )

    def join(half):
        drain(back_r.at[half], back_sem.at[half, 1])

        @pl.loop(0, EXPERTS)
        def _(e):
            ours, theirs = mine[half, e], back_r[half, e]
            whole[half, e, 0:12, :] = jnp.where(c == 0, ours, theirs)
            whole[half, e, 12:24, :] = jnp.where(c == 0, theirs, ours)

        held[half][0][0] = whole[half].astype(BF16)
        for copy in hop(half, 0):
            copy.start()

    def place_group(half, g):
        a, b = IN_GROUPS[g]
        if g:
            for copy in hop(half, g - 1):
                copy.wait_recv()
            if g < 4:
                for copy in hop(half, g):
                    copy.start()
        col = pl.multiple_of(x * 512 + c * 256 + half * 128, 128)

        @pl.loop(0, PLANE - 1)
        def _(index):
            px, py, pc = peer(index)
            e = plan[px, z * 8 + py * 2 + pc]
            picked[half, index, a:b] = held[half][g][:, e]
            remote(
                picked.at[half, index, a:b],
                result.at[a:b, y, :, pl.ds(col, 128)],
                spread_send.at[half],
                spread_recv.at[g],
                device(px, z, py, pc),
            ).start()

        result[a:b, y, :, pl.ds(col, 128)] = held[half][g][:, plan[x, z * 8 + y * 2 + c]]

    multiply(0)
    all_met(barrier)
    spread(0)
    multiply(1)
    spread(1)
    acc[PLANE] = jnp.zeros_like(acc[PLANE])
    for i in range(3):
        copies[2 + i].wait()

        @pl.loop(0, 4)
        def _(at):
            for e in range(EXPERTS):
                state[i, at, e] = loads[i][:, e, pl.ds(pl.multiple_of(at * 128, 128), 128)]

    for g in range(4):
        add_group(0, g)
    finish_sum(0)
    add_group(1, 0)
    update(0)
    add_group(1, 1)
    join(0)
    add_group(1, 2)
    place_group(0, 0)
    add_group(1, 3)
    place_group(0, 1)
    finish_sum(1)
    place_group(0, 2)
    update(1)
    place_group(0, 3)
    join(1)
    place_group(0, 4)
    for g in range(5):
        place_group(1, g)

    @pl.loop(0, 2)
    def _(half):
        ours = pl.multiple_of(c * 256 + half * 128, 128)
        theirs = pl.multiple_of((1 - c) * 256 + half * 128, 128)
        for e in range(EXPERTS):
            own[:, e, pl.ds(ours, 128)] = kept_grad[half, e]
            own[:, e, pl.ds(theirs, 128)] = swap_r[half, e]

    for g, (a, b) in enumerate(IN_GROUPS):
        drain(picked.at[:, pl.ds(0, PLANE - 1), a:b], spread_recv.at[g])
        for pos in range(a, b):
            away = (0, 7, 1, 6, 2, 5, 3, 4)[pos]
            pltpu.make_async_copy(result.at[pos], out.at[lax.rem(z + away, 8)], out_sem.at[pos]).start()
    for pos in range(8):
        drain(result.at[pos], out_sem.at[pos])
    for half in range(2):
        drain(swap_s.at[half], swap_sem.at[half, 0])
        drain(back_s.at[half], back_sem.at[half, 0])
        drain(pieces.at[half, pl.ds(0, PLANE - 1)], plane_send.at[half])
        drain(picked.at[half, pl.ds(0, PLANE - 1)], spread_send.at[half])
        for g in range(4):
            n = 12 if g == 0 else EXPERTS
            for ring, s in enumerate((up_s, down_s)):
                drain(s.at[half, g, pl.ds(0, n)], ring_send.at[half, ring, g])
        for k in range(4):
            for copy in hop(half, k):
                copy.wait_send()


VMEM = pl.BlockSpec(memory_space=pltpu.VMEM)
SMEM = pl.BlockSpec(memory_space=pltpu.SMEM)
ANY = pl.BlockSpec(memory_space=pl.ANY)
DMA = pltpu.SemaphoreType.DMA


def run_kernel(*operands):
    block = (24, 24, 128)
    exchange = pltpu.VMEM((2, 24, 12, 128), F32)
    return pl.pallas_call(
        kernel,
        out_shape=(
            jax.ShapeDtypeStruct((12, 24, 512), F32),
            jax.ShapeDtypeStruct((8, 4, 24, 2048), BF16),
        ),
        in_specs=[SMEM] * 4 + [ANY] * 5,
        out_specs=(VMEM, ANY),
        scratch_shapes=[
            pltpu.VMEM((1024, 768), BF16),
            pltpu.VMEM((1024, 2048), BF16),
            pltpu.VMEM((768, 1024), BF16),
            pltpu.VMEM((8, 4, 24, 2048), BF16),
            pltpu.VMEM((2, 32, 8, 24, 128), BF16),
            pltpu.VMEM((33, 8, 24, 128), F32),
        ]
        + [pltpu.VMEM((2, 4) + block, BF16)] * 4
        + [pltpu.VMEM((2,) + block, F32), exchange, exchange]
        + [pltpu.VMEM((12, 24, 512), F32)] * 3
        + [pltpu.VMEM((3, 4, 24, 12, 128), F32)]
        + [exchange] * 4
        + [pltpu.VMEM((2,) + block, F32)]
        + [pltpu.VMEM((b - a,) + block, BF16) for _ in range(2) for a, b in IN_GROUPS]
        + [
            pltpu.VMEM((2, 31, 8, 24, 128), BF16),
            pltpu.VMEM((8, 4, 24, 2048), BF16),
            DMA((5,)),
            DMA((2,)),
            DMA((2, 4)),
            DMA((2,)),
            DMA((2, 2, 4)),
            DMA((2, 2, 4)),
            DMA((2, 2)),
            DMA((2, 2)),
            DMA((2, 2, 4)),
            DMA((2, 2, 4)),
            DMA((2,)),
            DMA((5,)),
            DMA((8,)),
        ],
        compiler_params=pltpu.CompilerParams(
            collective_id=0, has_side_effects=True, vmem_limit_bytes=56 * 2**20
        ),
        name="sum_and_place",
    )(*operands)


def per_device(hidden_acts, out_grads, row_counts, plan_now, plan_next, master, moment_one, moment_two):
    z = lax.axis_index("expert") // 8
    ids = lax.dynamic_slice_in_dim(plan_now, z * 8, 8, axis=1).reshape(PLANE)
    order = jnp.arange(PLANE, dtype=jnp.int32)
    earlier = (ids[None, :] == ids[:, None]) & (order[None, :] < order[:, None])
    prev = jnp.max(jnp.where(earlier, order[None, :], -1), axis=1)
    prev = jnp.where(prev < 0, PLANE, prev)
    named = ids[None, :] == jnp.arange(EXPERTS, dtype=jnp.int32)[:, None]
    last = jnp.max(jnp.where(named, order[None, :], -1), axis=1)
    last = jnp.where(last < 0, PLANE, last)
    states = [jnp.swapaxes(array, 0, 1) for array in (master, moment_one, moment_two)]
    grad_sum, replica = run_kernel(
        row_counts, prev, last, plan_next, hidden_acts[0, 0], out_grads[0, 0], *states
    )
    news = [jnp.swapaxes(array, 0, 1) for array in adam(grad_sum, *states)]
    return (*news, replica.reshape(1, 1, 768, 2048))


def solution(mesh):
    state = P(None, "expert", "dp")
    split = P("dp", "expert", None, None)
    return jax.shard_map(
        per_device,
        mesh=mesh,
        in_specs=(split, split, P("dp", "expert"), P(), P(), state, state, state),
        out_specs=(state, state, state, split),
        check_vma=False,
    )
```

```python
import functools

import jax
import jax.numpy as jnp
from jax import lax
from jax.experimental import pallas as pl
from jax.experimental.pallas import tpu as pltpu
from jax.sharding import PartitionSpec as P

beta_one = 0.9
beta_two = 0.999
learn_rate = 0.1
epsilon = 1e-08
first_fix = 1.0 - beta_one**10
second_fix = 1.0 - beta_two**10

MESH = pl.DeviceIdType.MESH
BF16 = jnp.bfloat16
F32 = jnp.float32
EXPERTS = 24
PLANE = 32
OUT_GROUPS = ((0, 1), (1, 3), (3, 5), (5, 8))
IN_GROUPS = ((0, 1), (1, 3), (3, 5), (5, 7), (7, 8))


def place():
    o = lax.axis_index("expert")
    return lax.axis_index("dp"), o // 8, lax.rem(o // 2, 4), lax.rem(o, 2)


def device(x, z, y, c):
    return (x, z * 8 + y * 2 + c)


def wrap(value, size):
    return jnp.where(value >= size, value - size, value)


def each_peer(body):
    x, z, y, c = place()
    near = [wrap(x + dx, 4) for dx in range(4)]

    def four(j, count):
        far = jnp.where(j >= 4, j - 4, j)
        core = jnp.where(j >= 4, c, 1 - c)
        across = wrap(y + far, 4)
        for t in range(count):
            dx = (1 + 2 * t + t // 2) % 4
            body(4 * j + t, near[dx], wrap(across + (dx + 1) % 4, 4), core)

    @pl.loop(0, 7)
    def _(j):
        four(j, 4)

    four(jnp.int32(7), 3)


def meet():
    x, z, y, c = place()
    barrier = pltpu.get_barrier_semaphore()

    def greet(index, px, py, pc):
        pl.semaphore_signal(barrier, inc=1, device_id=device(px, z, py, pc), device_id_type=MESH)

    each_peer(greet)

    for step in (1, 7):
        pl.semaphore_signal(
            barrier, inc=1, device_id=device(x, lax.rem(z + step, 8), y, c), device_id_type=MESH
        )
    return barrier


def all_met(barrier):
    pl.semaphore_wait(barrier, PLANE + 1)


def remote(src, dst, send_sem, recv_sem, target):
    return pltpu.make_async_remote_copy(
        src_ref=src, dst_ref=dst, send_sem=send_sem, recv_sem=recv_sem, device_id=target, device_id_type=MESH
    )


def drain(ref, sem):
    pltpu.make_async_copy(ref, ref, sem).wait()


def adam(grad, weight, first, second):
    first = beta_one * first + (1.0 - beta_one) * grad
    second = beta_two * second + (1.0 - beta_two) * grad * grad
    step = learn_rate * (first / first_fix) / (jnp.sqrt(second / second_fix) + epsilon)
    return weight - step, first, second


def half_of(ring):
    return slice(12 * ring, 12 * ring + 12)


def kernel(
    count, prev, last, plan, hid_in, grd_in, weight_in, first_in, second_in, own, out,
    hid, grd, hid_t, part, pieces, acc, up_s, up_r, down_s, down_r, total, swap_s, swap_r,
    load_0, load_1, load_2, state, kept_grad, mine, back_s, back_r, whole,
    held_00, held_01, held_02, held_03, held_04, held_10, held_11, held_12, held_13, held_14,
    picked, result,
    load_sem, plane_send, plane_recv, self_sem, ring_send, ring_recv, swap_sem, back_sem,
    gather_send, gather_recv, spread_send, spread_recv, out_sem,
):
    held = ((held_00, held_01, held_02, held_03, held_04), (held_10, held_11, held_12, held_13, held_14))
    loads = (load_0, load_1, load_2)
    x, z, y, c = place()
    zplus, zminus = lax.rem(z + 1, 8), lax.rem(z + 7, 8)
    slot = (x * 4 + y) * 2 + c
    rows = hid.shape[0]
    copies = [pltpu.make_async_copy(hid_in, hid, load_sem.at[0]), pltpu.make_async_copy(grd_in, grd, load_sem.at[1])]
    for i, ref in enumerate((weight_in, first_in, second_in)):
        copies.append(pltpu.make_async_copy(ref, loads[i], load_sem.at[2 + i]))
    for copy in copies:
        copy.start()
    barrier = meet()
    live = lax.broadcasted_iota(jnp.int32, (256, 1), 0)
    copies[0].wait()

    for k in range(rows // 256):
        block = hid[k * 256 : (k + 1) * 256, :]
        kept = jnp.where(live + k * 256 < count[0, 0], block.astype(F32), 0.0)
        hid_t[:, k * 256 : (k + 1) * 256] = kept.T.astype(BF16)
    copies[1].wait()

    def multiply(half):
        for px in range(4):
            col = px * 512 + half * 128
            rhs = jnp.concatenate([grd[:, col : col + 128], grd[:, col + 256 : col + 384]], axis=1)
            out = jnp.dot(hid_t[...], rhs, preferred_element_type=F32)
            for dest in range(8):
                away = lax.rem(dest - z + 8, 8)
                pos = jnp.where(away == 0, 7, jnp.where(away < 4, 7 - 2 * away, 2 * (away - 4)))
                for py in range(4):
                    top = dest * 96 + py * 24
                    block = out[top : top + 24, :].astype(BF16)
                    part[pos, py, :, col : col + 128] = block[:, :128]
                    part[pos, py, :, col + 256 : col + 384] = block[:, 128:]

    def spread(half):
        for g, (a, b) in enumerate(OUT_GROUPS):

            def send(index, px, py, pc):
                col = pl.multiple_of(px * 512 + pc * 256 + half * 128, 128)
                remote(
                    part.at[a:b, py, :, pl.ds(col, 128)],
                    pieces.at[half, slot, a:b],
                    plane_send.at[half],
                    plane_recv.at[half, g],
                    device(px, z, py, pc),
                ).start()

            each_peer(send)

        col = pl.multiple_of(x * 512 + c * 256 + half * 128, 128)
        pltpu.make_async_copy(
            part.at[:, y, :, pl.ds(col, 128)], pieces.at[half, slot], self_sem.at[half]
        ).start()

    def add_group(half, g):
        a, b = OUT_GROUPS[g]
        if g == 0:
            drain(pieces.at[half, 0], self_sem.at[half])
        drain(pieces.at[half, pl.ds(0, PLANE - 1), a:b], plane_recv.at[half, g])

        @pl.loop(0, PLANE)
        def _(i):
            acc[i, a:b] = pieces[half, i, a:b].astype(F32) + acc[prev[i], a:b]

        if g == 0:

            @pl.loop(0, EXPERTS // 2)
            def _(e):
                up_s[half, 0, e] = acc[last[e], 0].astype(BF16)
                down_s[half, 0, e] = acc[last[e + 12], 0].astype(BF16)

        else:
            for ring, (buf, r) in enumerate(((up_s, up_r), (down_s, down_r))):
                first = half_of(ring) if g == 1 else slice(0, EXPERTS)
                n = first.stop - first.start
                drain(r.at[half, g - 1, pl.ds(0, n)], ring_recv.at[half, ring, g - 1])
                pos = a + ring

                @pl.loop(0, n)
                def _(e):
                    buf[half, g, e + first.start] = (
                        acc[last[e + first.start], pos] + r[half, g - 1, e].astype(F32)
                    ).astype(BF16)

                if g == 1:

                    @pl.loop(0, EXPERTS - n)
                    def _(e):
                        other = e + (12 - first.start)
                        buf[half, g, other] = acc[last[other], pos].astype(BF16)

        n = 12 if g == 0 else EXPERTS
        for ring, (s, r, to) in enumerate(((up_s, up_r, zplus), (down_s, down_r, zminus))):
            remote(
                s.at[half, g, pl.ds(0, n)],
                r.at[half, g, pl.ds(0, n)],
                ring_send.at[half, ring, g],
                ring_recv.at[half, ring, g],
                device(x, to, y, c),
            ).start()

    def finish_sum(half):
        for ring, r in enumerate((up_r, down_r)):
            drain(r.at[half, 3], ring_recv.at[half, ring, 3])

        @pl.loop(0, EXPERTS)
        def _(e):
            total[half, e] = acc[last[e], 7] + up_r[half, 3, e].astype(F32) + down_r[half, 3, e].astype(F32)

        @pl.loop(0, EXPERTS)
        def _(e):
            low, high = total[half, e, 0:12, :], total[half, e, 12:24, :]
            kept_grad[half, e] = jnp.where(c == 0, low, high)
            swap_s[half, e] = jnp.where(c == 0, high, low)

        remote(
            swap_s.at[half], swap_r.at[half], swap_sem.at[half, 0], swap_sem.at[half, 1], device(x, z, y, 1 - c)
        ).start()

        @pl.loop(0, EXPERTS)
        def _(e):
            at = 2 * c + half
            mine[half, e] = adam(kept_grad[half, e], state[0, at, e], state[1, at, e], state[2, at, e])[0]

    def update(half):
        drain(swap_r.at[half], swap_sem.at[half, 1])

        @pl.loop(0, EXPERTS)
        def _(e):
            at = 2 * (1 - c) + half
            back_s[half, e] = adam(swap_r[half, e], state[0, at, e], state[1, at, e], state[2, at, e])[0]

        remote(
            back_s.at[half], back_r.at[half], back_sem.at[half, 0], back_sem.at[half, 1], device(x, z, y, 1 - c)
        ).start()

    def hop(half, k):
        for ring, to in enumerate((zplus, zminus)):
            src = 0 if k == 0 else ring
            dst = 0 if k == 3 else ring
            piece = pl.ds(12 * ring, 12) if k == 3 else pl.ds(0, EXPERTS)
            yield remote(
                held[half][k].at[src, piece],
                held[half][k + 1].at[dst, piece],
                gather_send.at[half, ring, k],
                gather_recv.at[half, ring, k],
                device(x, to, y, c),
            )

    def join(half):
        drain(back_r.at[half], back_sem.at[half, 1])

        @pl.loop(0, EXPERTS)
        def _(e):
            ours, theirs = mine[half, e], back_r[half, e]
            whole[half, e, 0:12, :] = jnp.where(c == 0, ours, theirs)
            whole[half, e, 12:24, :] = jnp.where(c == 0, theirs, ours)

        held[half][0][0] = whole[half].astype(BF16)
        for copy in hop(half, 0):
            copy.start()

    def place_group(half, g):
        a, b = IN_GROUPS[g]
        if g:
            for copy in hop(half, g - 1):
                copy.wait_recv()
            if g < 4:
                for copy in hop(half, g):
                    copy.start()
        col = pl.multiple_of(x * 512 + c * 256 + half * 128, 128)

        def send(index, px, py, pc):
            e = plan[px, z * 8 + py * 2 + pc]
            picked[half, index, a:b] = held[half][g][:, e]
            remote(
                picked.at[half, index, a:b],
                result.at[a:b, y, :, pl.ds(col, 128)],
                spread_send.at[half],
                spread_recv.at[g],
                device(px, z, py, pc),
            ).start()

        each_peer(send)
        result[a:b, y, :, pl.ds(col, 128)] = held[half][g][:, plan[x, z * 8 + y * 2 + c]]

    multiply(0)
    all_met(barrier)
    spread(0)
    multiply(1)
    spread(1)
    acc[PLANE] = jnp.zeros_like(acc[PLANE])
    for i in range(3):
        copies[2 + i].wait()

        @pl.loop(0, 4)
        def _(at):
            for e in range(EXPERTS):
                state[i, at, e] = loads[i][:, e, pl.ds(pl.multiple_of(at * 128, 128), 128)]

    for g in range(4):
        add_group(0, g)
    finish_sum(0)
    add_group(1, 0)
    update(0)
    add_group(1, 1)
    join(0)
    add_group(1, 2)
    place_group(0, 0)
    add_group(1, 3)
    place_group(0, 1)
    finish_sum(1)
    place_group(0, 2)
    update(1)
    place_group(0, 3)
    join(1)
    place_group(0, 4)
    for g in range(5):
        place_group(1, g)

    @pl.loop(0, 2)
    def _(half):
        ours = pl.multiple_of(c * 256 + half * 128, 128)
        theirs = pl.multiple_of((1 - c) * 256 + half * 128, 128)
        for e in range(EXPERTS):
            own[:, e, pl.ds(ours, 128)] = kept_grad[half, e]
            own[:, e, pl.ds(theirs, 128)] = swap_r[half, e]

    for g, (a, b) in enumerate(IN_GROUPS):
        drain(picked.at[:, pl.ds(0, PLANE - 1), a:b], spread_recv.at[g])
        for pos in range(a, b):
            away = (0, 7, 1, 6, 2, 5, 3, 4)[pos]
            pltpu.make_async_copy(result.at[pos], out.at[lax.rem(z + away, 8)], out_sem.at[pos]).start()
    for pos in range(8):
        drain(result.at[pos], out_sem.at[pos])
    for half in range(2):
        drain(swap_s.at[half], swap_sem.at[half, 0])
        drain(back_s.at[half], back_sem.at[half, 0])
        drain(pieces.at[half, pl.ds(0, PLANE - 1)], plane_send.at[half])
        drain(picked.at[half, pl.ds(0, PLANE - 1)], spread_send.at[half])
        for g in range(4):
            n = 12 if g == 0 else EXPERTS
            for ring, s in enumerate((up_s, down_s)):
                drain(s.at[half, g, pl.ds(0, n)], ring_send.at[half, ring, g])
        for k in range(4):
            for copy in hop(half, k):
                copy.wait_send()


VMEM = pl.BlockSpec(memory_space=pltpu.VMEM)
SMEM = pl.BlockSpec(memory_space=pltpu.SMEM)
ANY = pl.BlockSpec(memory_space=pl.ANY)
DMA = pltpu.SemaphoreType.DMA


def run_kernel(*operands):
    block = (24, 24, 128)
    exchange = pltpu.VMEM((2, 24, 12, 128), F32)
    return pl.pallas_call(
        kernel,
        out_shape=(
            jax.ShapeDtypeStruct((12, 24, 512), F32),
            jax.ShapeDtypeStruct((8, 4, 24, 2048), BF16),
        ),
        in_specs=[SMEM] * 4 + [ANY] * 5,
        out_specs=(VMEM, ANY),
        scratch_shapes=[
            pltpu.VMEM((1024, 768), BF16),
            pltpu.VMEM((1024, 2048), BF16),
            pltpu.VMEM((768, 1024), BF16),
            pltpu.VMEM((8, 4, 24, 2048), BF16),
            pltpu.VMEM((2, 32, 8, 24, 128), BF16),
            pltpu.VMEM((33, 8, 24, 128), F32),
        ]
        + [pltpu.VMEM((2, 4) + block, BF16)] * 4
        + [pltpu.VMEM((2,) + block, F32), exchange, exchange]
        + [pltpu.VMEM((12, 24, 512), F32)] * 3
        + [pltpu.VMEM((3, 4, 24, 12, 128), F32)]
        + [exchange] * 4
        + [pltpu.VMEM((2,) + block, F32)]
        + [pltpu.VMEM((b - a,) + block, BF16) for _ in range(2) for a, b in IN_GROUPS]
        + [
            pltpu.VMEM((2, 31, 8, 24, 128), BF16),
            pltpu.VMEM((8, 4, 24, 2048), BF16),
            DMA((5,)),
            DMA((2,)),
            DMA((2, 4)),
            DMA((2,)),
            DMA((2, 2, 4)),
            DMA((2, 2, 4)),
            DMA((2, 2)),
            DMA((2, 2)),
            DMA((2, 2, 4)),
            DMA((2, 2, 4)),
            DMA((2,)),
            DMA((5,)),
            DMA((8,)),
        ],
        compiler_params=pltpu.CompilerParams(
            collective_id=0, has_side_effects=True, vmem_limit_bytes=56 * 2**20
        ),
        name="sum_and_place",
    )(*operands)


def per_device(hidden_acts, out_grads, row_counts, plan_now, plan_next, master, moment_one, moment_two):
    z = lax.axis_index("expert") // 8
    ids = lax.dynamic_slice_in_dim(plan_now, z * 8, 8, axis=1).reshape(PLANE)
    order = jnp.arange(PLANE, dtype=jnp.int32)
    earlier = (ids[None, :] == ids[:, None]) & (order[None, :] < order[:, None])
    prev = jnp.max(jnp.where(earlier, order[None, :], -1), axis=1)
    prev = jnp.where(prev < 0, PLANE, prev)
    named = ids[None, :] == jnp.arange(EXPERTS, dtype=jnp.int32)[:, None]
    last = jnp.max(jnp.where(named, order[None, :], -1), axis=1)
    last = jnp.where(last < 0, PLANE, last)
    states = [jnp.swapaxes(array, 0, 1) for array in (master, moment_one, moment_two)]
    grad_sum, replica = run_kernel(
        row_counts, prev, last, plan_next, hidden_acts[0, 0], out_grads[0, 0], *states
    )
    news = [jnp.swapaxes(array, 0, 1) for array in adam(grad_sum, *states)]
    return (*news, replica.reshape(1, 1, 768, 2048))


def solution(mesh):
    state = P(None, "expert", "dp")
    split = P("dp", "expert", None, None)
    return jax.shard_map(
        per_device,
        mesh=mesh,
        in_specs=(split, split, P("dp", "expert"), P(), P(), state, state, state),
        out_specs=(state, state, state, split),
        check_vma=False,
    )
```
